32 devices in a mesh: row: 4 (over z), col: 4 (over x, core), depth: 2 (over y).
Axes of the slice: x: 2, y: 2, z: 4, core: 2. Of those that a mesh axis runs over, the one named last changes fastest.
Arguments:
- amplitudes: float32 [14400, 4, 1200], P('row', 'depth', 'col'), may hold values from -6 to 6
- integrals: float32 [4, 1200, 4, 1200], P('depth', 'row', 'col'), may hold values from -0.375 to 0.375
- occ_energy: float32 [120], replicated, may hold values from -2 to -0.5
- vir_energy: float32 [1200], replicated, may hold values from 0.3 to 3
Outputs:
- update: float32 [14400, 4, 1200], P(('row', 'col'), 'depth')
The draws below stay inside these ranges and needn't reach their ends.
All inputs are finite; a program needn't handle non-finite values.
Results may differ from the reference program's by a relative error of at most 0.00007.
Values sent between devices are 32-bit elements; how exact they have to be, the bound alone decides.
A program may use at most 192 MiB of HBM per device.

```python
import jax
import jax.numpy as jnp
from jax import lax

NOCC = 120
NVIR = 1200
AB = 4
PANELS = 4
NPAIR = 14400


def steps_of(own_key, dims, split, low, top_value):
    def one(axis_at, parts):
        steps = jax.random.uniform(jax.random.fold_in(jax.random.fold_in(own_key, 6), axis_at), (parts,), jnp.float32, low / len(split), top_value / len(split))
        return jnp.repeat(jnp.exp(steps), dims[axis_at] // parts).reshape((-1,) + (1,) * (len(dims) - axis_at - 1))

    gain = one(*split[0])
    for cut in split[1:]:
        gain = gain * one(*cut)
    return gain


def normal_values(own_key, dims, deviation, reach, shards=(), dtype=jnp.bfloat16):
    result = jax.random.normal(own_key, dims, jnp.float32) * deviation
    if len(shards) > 0:
        result = steps_of(own_key, dims, shards, -0.22, 0.18) * result
    return jnp.clip(result, min=-reach, max=reach).astype(dtype)


def setup_inputs(seed: int = 0) -> dict:
    key_of = jax.random.split(jax.random.key(seed), 5)
    return {
        "amplitudes": normal_values(key_of[0], (NPAIR, PANELS, NVIR), 1.0, 6.0, ((0, 4), (1, 2), (2, 4)), jnp.float32),
        "integrals": normal_values(key_of[1], (PANELS, NVIR, AB, NVIR), (PANELS * NVIR // 16) ** -0.5, 0.375, ((0, 2), (1, 4), (2, 4)), jnp.float32),
        "occ_energy": jnp.clip(jax.random.uniform(key_of[2], (NOCC,), jnp.float32, -2.0, -0.5), -2.0, -0.5),
        "vir_energy": jnp.clip(jax.random.uniform(key_of[3], (NVIR,), jnp.float32, 0.3, 3.0), 0.3, 3.0),
    }


def reference(amplitudes, integrals, occ_energy, vir_energy):
    left = amplitudes.reshape(NPAIR, PANELS * NVIR)
    right = integrals.reshape(PANELS * NVIR, AB * NVIR)
    ladder = jnp.dot(left, right, precision=lax.Precision.HIGHEST, preferred_element_type=jnp.float32)
    ladder = ladder.reshape(NPAIR, AB, NVIR)
    pair_energy = (occ_energy[:, None] + occ_energy[None, :]).reshape(NPAIR)
    denominator = pair_energy[:, None, None] - vir_energy[:AB][None, :, None] - vir_energy[None, None, :]
    return ladder / denominator
```

```python
import jax
import jax.numpy as jnp
from jax import lax
from jax.experimental.layout import Layout, with_layout_constraint
from jax.sharding import PartitionSpec as P


def make_body(mesh):
    rows_n, cols_n, depth_n = mesh.shape["row"], mesh.shape["col"], mesh.shape["depth"]
    assert cols_n % 4 == 0 and depth_n == 2 and rows_n % cols_n == 0
    split = rows_n // cols_n
    chips_x = cols_n // 2
    lows = chips_x // 2

    def flip_col(value, bits):
        return lax.ppermute(value, "col", [(i, i ^ bits) for i in range(cols_n)])

    def flip_row(value, bits):
        return lax.ppermute(value, "row", [(i, i ^ bits) for i in range(rows_n)])

    def flip_depth(value):
        return lax.ppermute(value, "depth", [(0, 1), (1, 0)])

    def turn(value):
        pairs = []
        for high in range(2):
            for low in range(lows):
                for core in range(2):
                    for y in range(2):
                        source = ((high * lows + low) * 2 + core) * 2 + y
                        pairs.append((source, ((y * lows + low) * 2 + core) * 2 + high))
        return lax.ppermute(value, ("col", "depth"), pairs)

    def row_major(value):
        return with_layout_constraint(value, Layout(major_to_minor=tuple(range(value.ndim))))

    def body(amplitudes, integrals, occ_energy, vir_energy):
        row, col, y = lax.axis_index("row"), lax.axis_index("col"), lax.axis_index("depth")
        x, core = col // 2, col % 2
        panels, d_rows, a_own, b_count = integrals.shape
        pair_rows, _, d_cols = amplitudes.shape
        pairs = pair_rows // cols_n

        own = integrals.reshape(panels * d_rows, a_own * b_count)
        first_piece = turn(own)
        pieces = [[first_piece] + [flip_row(first_piece, s) for s in range(1, rows_n)]]
        for t in range(1, chips_x):
            start = flip_col(pieces[0][0], 2 * t)
            pieces.append([start, flip_row(start, 1)])
            pieces[t] += [flip_col(pieces[0][s], 2 * t) for s in range(2, rows_n)]

        quarters = row_major(amplitudes.reshape(cols_n, pairs, panels * d_cols))
        mine = []
        for s in range(cols_n):
            piece = lax.dynamic_index_in_dim(quarters, col ^ s, 0, keepdims=False)
            mine.append(piece if s == 0 else flip_col(piece, s))
        theirs = [flip_depth(piece) for piece in mine]
        table = row_major(jnp.stack(mine + theirs))

        def left(panel_group, d_block):
            at = (panel_group ^ y) * cols_n + ((d_block // split) ^ col)
            piece = lax.dynamic_index_in_dim(table, at, 0, keepdims=False)
            if split > 1:
                piece = piece.reshape(pairs, panels, d_cols)
                piece = lax.dynamic_slice_in_dim(piece, (d_block % split) * d_rows, d_rows, 2)
                piece = piece.reshape(pairs, panels * d_rows)
            return piece

        totals = [None] * (2 * lows)
        for s in range(rows_n):
            for t in range(chips_x):
                lhs = left((x ^ t) // lows, row ^ s)
                for flip in range(2):
                    rhs = pieces[t][s] if flip == 0 else flip_col(pieces[t][s], 1)
                    part = jnp.dot(
                        lhs, rhs, precision=lax.Precision.HIGH, preferred_element_type=jnp.float32
                    )
                    at = (t % lows) * 2 + flip
                    if totals[at] is not None:
                        part = totals[at] + part
                    totals[at] = lax.optimization_barrier(part)

        here = (x % lows) * 2 + core
        by_a = []
        for a in range(2 * lows):
            value = totals[a]
            for other in range(2 * lows):
                if other != a:
                    value = jnp.where(here == (a ^ other), totals[other], value)
            by_a.append(value)
        ladder = jnp.stack(by_a, axis=1).reshape(pairs, 2 * lows * a_own, b_count)

        occ_count = occ_energy.shape[0]
        pair_index = (row * cols_n + col) * pairs + jnp.arange(pairs, dtype=jnp.int32)
        occ_ids = jnp.arange(occ_count, dtype=jnp.int32)
        first = jnp.sum(
            jnp.where((pair_index // occ_count)[:, None] == occ_ids[None, :], occ_energy[None, :], 0.0),
            axis=1,
        )
        second = jnp.sum(
            jnp.where((pair_index % occ_count)[:, None] == occ_ids[None, :], occ_energy[None, :], 0.0),
            axis=1,
        )
        batch = lax.dynamic_slice_in_dim(vir_energy, y * ladder.shape[1], ladder.shape[1])
        denominator = (first + second)[:, None, None] - batch[None, :, None] - vir_energy[None, None, :]
        return ladder / denominator

    return body


def solution(mesh):
    in_specs = (P("row", "depth", "col"), P("depth", "row", "col", None), P(), P())
    out_specs = P(("row", "col"), "depth", None)
    return jax.shard_map(
        make_body(mesh), mesh=mesh, in_specs=in_specs, out_specs=out_specs, check_vma=False
    )
```

```python
import jax
import jax.numpy as jnp
from jax import lax
from jax.experimental.layout import Layout, with_layout_constraint
from jax.sharding import PartitionSpec as P


def make_body(mesh):
    rows_n, cols_n, depth_n = mesh.shape["row"], mesh.shape["col"], mesh.shape["depth"]
    assert cols_n % 4 == 0 and depth_n == 2 and rows_n % cols_n == 0
    split = rows_n // cols_n
    chips_x = cols_n // 2
    lows = chips_x // 2

    def flip_col(value, bits):
        return lax.ppermute(value, "col", [(i, i ^ bits) for i in range(cols_n)])

    def shift_row(value, step):
        return lax.ppermute(value, "row", [(i, (i + step) % rows_n) for i in range(rows_n)])

    def ring(value):
        gathered = [None] * rows_n
        gathered[0] = value
        up, down = value, value
        half = rows_n // 2
        for hop in range(1, half):
            up = shift_row(up, 1)
            down = shift_row(down, -1)
            gathered[rows_n - hop], gathered[hop] = up, down
        cut = (value.shape[0] // 2 + 7) // 8 * 8
        top = shift_row(up[:cut], 1)
        bottom = shift_row(down[cut:], -1)
        gathered[half] = jnp.concatenate([top, bottom], axis=0)
        return gathered

    def flip_depth(value):
        return lax.ppermute(value, "depth", [(0, 1), (1, 0)])

    def turn(value):
        pairs = []
        for high in range(2):
            for low in range(lows):
                for core in range(2):
                    for y in range(2):
                        source = ((high * lows + low) * 2 + core) * 2 + y
                        pairs.append((source, ((y * lows + low) * 2 + core) * 2 + high))
        return lax.ppermute(value, ("col", "depth"), pairs)

    def row_major(value):
        return with_layout_constraint(value, Layout(major_to_minor=tuple(range(value.ndim))))

    def body(amplitudes, integrals, occ_energy, vir_energy):
        row, col, y = lax.axis_index("row"), lax.axis_index("col"), lax.axis_index("depth")
        x, core = col // 2, col % 2
        panels, d_rows, a_own, b_count = integrals.shape
        pair_rows, _, d_cols = amplitudes.shape
        pairs = pair_rows // cols_n

        own = integrals.reshape(panels * d_rows, a_own * b_count)
        first_piece = turn(own)
        pieces = []
        for t in range(chips_x):
            start = first_piece if t == 0 else flip_col(first_piece, 2 * t)
            pieces.append(ring(start))

        quarters = row_major(amplitudes.reshape(cols_n, pairs, panels * d_cols))
        mine = []
        for s in range(cols_n):
            piece = lax.dynamic_index_in_dim(quarters, col ^ s, 0, keepdims=False)
            mine.append(piece if s == 0 else flip_col(piece, s))
        theirs = []
        for piece in mine:
            theirs.append(flip_depth(piece))
        table = row_major(jnp.stack(mine + theirs))

        def left(panel_group, d_block):
            at = (panel_group ^ y) * cols_n + ((d_block // split) ^ col)
            piece = lax.dynamic_index_in_dim(table, at, 0, keepdims=False)
            if split > 1:
                piece = piece.reshape(pairs, panels, d_cols)
                piece = lax.dynamic_slice_in_dim(piece, (d_block % split) * d_rows, d_rows, 2)
                piece = piece.reshape(pairs, panels * d_rows)
            return piece

        totals = [None] * (2 * lows)
        order = sorted(range(rows_n), key=lambda s: min(s, rows_n - s))
        for t in range(chips_x):
            for s in order:
                lhs = left((x ^ t) // lows, (row + s) % rows_n)
                for flip in range(2):
                    rhs = pieces[t][s] if flip == 0 else flip_col(pieces[t][s], 1)
                    part = jnp.dot(
                        lhs, rhs, precision=lax.Precision.HIGH, preferred_element_type=jnp.float32
                    )
                    at = (t % lows) * 2 + flip
                    if totals[at] is not None:
                        part = totals[at] + part
                    totals[at] = lax.optimization_barrier(part)

        here = (x % lows) * 2 + core
        by_a = []
        for a in range(2 * lows):
            value = totals[a]
            for other in range(2 * lows):
                if other != a:
                    value = jnp.where(here == (a ^ other), totals[other], value)
            by_a.append(value)
        ladder = jnp.stack(by_a, axis=1).reshape(pairs, 2 * lows * a_own, b_count)

        occ_count = occ_energy.shape[0]
        pair_index = (row * cols_n + col) * pairs + jnp.arange(pairs, dtype=jnp.int32)
        occ_ids = jnp.arange(occ_count, dtype=jnp.int32)
        first = jnp.sum(
            jnp.where((pair_index // occ_count)[:, None] == occ_ids[None, :], occ_energy[None, :], 0.0),
            axis=1,
        )
        second = jnp.sum(
            jnp.where((pair_index % occ_count)[:, None] == occ_ids[None, :], occ_energy[None, :], 0.0),
            axis=1,
        )
        batch = lax.dynamic_slice_in_dim(vir_energy, y * ladder.shape[1], ladder.shape[1])
        denominator = (first + second)[:, None, None] - batch[None, :, None] - vir_energy[None, None, :]
        return ladder / denominator

    return body


def solution(mesh):
    in_specs = (P("row", "depth", "col"), P("depth", "row", "col", None), P(), P())
    out_specs = P(("row", "col"), "depth", None)
    body = make_body(mesh)

    return jax.shard_map(body, mesh=mesh, in_specs=in_specs, out_specs=out_specs, check_vma=False)
```
